512 devices in a mesh: row: 16 (over y_lo, x, core), col: 32 (over y_hi, z).
Axes of the slice: x: 4, y: 8 (y_hi: 4, y_lo: 2; y = y_hi * 2 + y_lo), z: 8, core: 2. Of those that a mesh axis runs over, the one named last changes fastest.
Arguments:
- vectors: float32 [2048, 16384], P('row', 'col'), may hold values from -6 to 6
- factors: float32 [32, 4, 512, 512], P('col', None, 'row'), may hold values from -1 to 1, as said below
- offsets: int32 [32], replicated, may hold values from 0 to 1
Outputs:
- updated: float32 [2048, 16384], P('row', 'col')
The draws below stay inside these ranges and needn't reach their ends.
Inputs may be any that keep to these rules, and one draw needn't show every extreme that they name: Each factors[c, k] is an orthogonal matrix.
All inputs are finite; a program needn't handle non-finite values.
Results may differ from the reference program's by a relative error of at most 0.00014.
Values sent between devices are 32-bit elements; how exact they have to be, the bound alone decides.
A program may use at most 64 MiB of HBM per device.

```python
import jax
import jax.numpy as jnp
from jax import lax

F = 512
NROWS = 2048
WIN = 16384
CHAINS = 32


def draw_factors(key, part):
    sample = jax.random.normal(key, (CHAINS * 4, F, F), jnp.float32)
    orthogonal, upper_tri = jnp.linalg.qr(sample)
    return orthogonal.reshape(CHAINS, 4, F, F)


def plant(array, key, least, high):
    longest = array.shape.index(max(array.shape))
    spots = []
    for shift in (0, 1):
        where = [jax.random.randint(jax.random.fold_in(key, axis), (), 0, length) for axis, length in enumerate(array.shape)]
        where[longest] = (where[longest] + shift) % array.shape[longest]
        spots.append(tuple(where))
    return array.at[spots[0]].set(least).at[spots[1]].set(high)


def block_levels(own_key, extent, shards, smallest, top_value):
    def one(position, shards_of):
        heights = jax.random.uniform(jax.random.fold_in(jax.random.fold_in(own_key, 6), position), (shards_of,), jnp.float32, smallest / len(shards), top_value / len(shards))
        return jnp.repeat(jnp.exp(heights), extent[position] // shards_of).reshape((-1,) + (1,) * (len(extent) - position - 1))

    loudness = one(*shards[0])
    for cut in shards[1:]:
        loudness = loudness * one(*cut)
    return loudness


def bell_draw(stream_key, shape, deviation, reach, cuts=(), held_as=jnp.bfloat16):
    result = deviation * jax.random.normal(stream_key, shape, jnp.float32)
    if cuts:
        result = result * block_levels(stream_key, shape, cuts, -0.22, 0.18)
    return jnp.clip(result, -reach, reach).astype(held_as)


def setup_inputs(seed: int = 0) -> dict:
    key_list = jax.random.split(jax.random.key(seed), 4)
    return {
        "vectors": bell_draw(key_list[0], (NROWS, WIN), 1.0, 6.0, ((0, 16), (1, 32)), jnp.float32),
        "factors": draw_factors(jax.random.fold_in(key_list[3], 71), 0),
        "offsets": plant(jax.random.randint(key_list[2], (CHAINS,), 0, 2), jax.random.fold_in(key_list[2], 1), 0, 1).astype(jnp.int32),
    }


def apply_chain(section, chain_factors, stride, first_col, width):
    identity = jnp.eye(2 * stride, dtype=jnp.float32)
    for factor_no in range(4):
        valid = first_col + factor_no * stride + 2 * stride <= width
        factor = jnp.where(valid, chain_factors[factor_no], identity)
        before = section[:, :factor_no * stride]
        middle = section[:, factor_no * stride:factor_no * stride + 2 * stride]
        beyond = section[:, factor_no * stride + 2 * stride:]
        middle = jnp.dot(middle.astype(jnp.float32), factor.astype(jnp.float32), precision=lax.Precision.HIGHEST, preferred_element_type=jnp.float32)
        section = jnp.concatenate([before, middle, beyond], 1)
    return section

def reference(vectors, factors, offsets):
    stride = F // 2
    width = vectors.shape[1]
    updated = jnp.concatenate([vectors, jnp.zeros((vectors.shape[0], 4 * stride), jnp.float32)], 1)
    for tick_num in range(3):
        for chain_no in range(tick_num, CHAINS, 3):
            first_col = (chain_no * F + offsets[chain_no] * stride).astype(jnp.int32)
            section = lax.dynamic_slice_in_dim(updated, first_col, 5 * stride, 1)
            section = apply_chain(section, factors[chain_no], stride, first_col, width)
            updated = lax.dynamic_update_slice_in_dim(updated, section, first_col, 1)
    return updated[:, :width]
```

```python
import functools

import jax
import jax.numpy as jnp
from jax import lax
from jax.experimental import pallas as pl
from jax.experimental.pallas import tpu as pltpu
from jax.sharding import PartitionSpec as P

MESH = pl.DeviceIdType.MESH


def kernel(groups, vec, fac, off, out, fetched, gather, hop, whi, wlo, own, one, two, right1, right2, left, last,
           gsend, grecv, ssend, srecv, zsend, zrecv, vsend, vrecv, fsem):
    row = lax.axis_index("row")
    col = lax.axis_index("col")
    half = own.shape[2]
    core = lax.rem(row, 2)
    chip = row // 2
    x = lax.rem(chip, 4)
    y = chip // 4
    place = lax.rem(col, 3)
    has_left = col > 0
    has_right = col < groups - 1
    xnext = y * 4 + lax.rem(x + 1, 4)
    xprev = y * 4 + lax.rem(x + 3, 4)
    xfar = y * 4 + lax.rem(x + 2, 4)
    other = (1 - y) * 4
    ychip = other + x
    sibling = chip * 2 + (1 - core)

    fetches = [
        pltpu.make_async_copy(fac, fetched, fsem.at[0]),
        pltpu.make_async_copy(vec.at[:, pl.ds(0, half)], own.at[0], fsem.at[1]),
        pltpu.make_async_copy(vec.at[:, pl.ds(half, half)], own.at[1], fsem.at[2]),
    ]
    for fetch in fetches:
        fetch.start()

    barrier = pltpu.get_barrier_semaphore()

    def greet(r, c):
        pl.semaphore_signal(barrier, inc=1, device_id=(r, c), device_id_type=MESH)

    for c in (xnext, xprev, ychip):
        greet(c * 2 + core, col)
    greet(sibling, col)

    @pl.when(has_left)
    def _():
        greet(row, col - 1)

    @pl.when(has_right)
    def _():
        greet(row, col + 1)

    for fetch in fetches:
        fetch.wait()
    shift = off[col] > 0
    f0, f1, f2, f3 = fetched[0, 0], fetched[0, 1], fetched[0, 2], fetched[0, 3]
    gather[0, chip, core] = f0
    gather[1, chip, core] = jnp.where(shift, f0, f1)
    hop[0] = jnp.where(shift, f1, f2)
    hop[1] = jnp.where(shift, f2, f3)
    hop[2] = f3

    pl.semaphore_wait(barrier, 4 + has_left.astype(jnp.int32) + has_right.astype(jnp.int32))

    def hop_copy(i):
        return pltpu.make_async_remote_copy(
            hop.at[i], gather.at[i + 2, chip, core], zsend.at[i], zrecv.at[i],
            device_id=(row, col + 1), device_id_type=MESH)

    @pl.when(has_right)
    def _():
        for i in range(3):
            hop_copy(i).start()

    def vcopy(src, dst, slot, landing, to):
        return pltpu.make_async_remote_copy(
            src, dst, vsend.at[slot], vrecv.at[landing], device_id=(row, to), device_id_type=MESH)

    def loan_half():
        return vcopy(own.at[0], right1.at[0], 0, 0, col - 1)

    def loan_block():
        return vcopy(own, right1, 0, 0, col - 1)

    @pl.when(place == 1)
    def _():
        loan_half().start()

    @pl.when(place == 2)
    def _():
        loan_block().start()

    def shard(f, s, to, slot):
        return pltpu.make_async_remote_copy(
            gather.at[f, s, core], gather.at[f, s, core], gsend.at[f, slot], grecv.at[f, s],
            device_id=(to * 2 + core, col), device_id_type=MESH)

    def got(f, s):
        shard(f, s, xnext, 0).wait_recv()

    def step_one(f):
        @pl.when(f >= 2)
        def _():
            hop_copy(f - 2).wait_recv()

        shard(f, chip, ychip, 0).start()
        shard(f, chip, xnext, 1).start()
        shard(f, chip, xprev, 2).start()

    def step_two(f):
        @pl.when(core == 0)
        def _():
            up = lax.rem(f, 2) == 0
            got(f, xprev)
            shard(f, xprev, ychip, 3).start()

            @pl.when(up)
            def _():
                shard(f, xprev, xnext, 4).start()

            got(f, xnext)
            shard(f, xnext, ychip, 5).start()

            @pl.when(jnp.logical_not(up))
            def _():
                shard(f, xnext, xprev, 4).start()

        @pl.when(core == 1)
        def _():
            got(f, ychip)
            shard(f, ychip, xnext, 3).start()
            shard(f, ychip, xprev, 4).start()
            got(f, xprev)
            shard(f, xprev, xnext, 5).start()

    def step_three(f):
        @pl.when(core == 0)
        def _():
            got(f, xfar)
            shard(f, xfar, ychip, 6).start()

        @pl.when(core == 1)
        def _():
            relayed = other + lax.rem(x + 1, 4)
            got(f, relayed)
            shard(f, relayed, xprev, 6).start()

    def to_sibling(f):
        return pltpu.make_async_remote_copy(
            gather.at[f, :, core], gather.at[f, :, core], ssend.at[f], srecv.at[f],
            device_id=(sibling, col), device_id_type=MESH)

    def from_sibling(f):
        return pltpu.make_async_remote_copy(
            gather.at[f, :, 1 - core], gather.at[f, :, 1 - core], ssend.at[f], srecv.at[f],
            device_id=(sibling, col), device_id_type=MESH)

    def step_four(f):
        @pl.when(core == 0)
        def _():
            for i in range(4):
                got(f, other + i)

        @pl.when(core == 1)
        def _():
            got(f, xnext)
            got(f, xfar)
            got(f, other + lax.rem(x + 2, 4))
            got(f, other + lax.rem(x + 3, 4))

        to_sibling(f).start()

    def step_five(f):
        from_sibling(f).wait_recv()

        def split(i, carry):
            for k in range(2):
                g = gather[f, i, k]
                hi = g.astype(jnp.bfloat16)
                whi[f, 2 * i + k] = hi
                wlo[f, 2 * i + k] = (g - hi.astype(jnp.float32)).astype(jnp.bfloat16)
            return carry

        lax.fori_loop(0, 8, split, 0)

    def each(step, lo, hi):
        def body(f, carry):
            step(f)
            return carry

        lax.fori_loop(lo, hi, body, 0)

    wide = 2 * half
    hr = has_right.astype(jnp.int32)
    keep_first = 1 - off[col]
    keep_fifth = hr * off[jnp.maximum(col - 1, 0)]

    def products(work, lo, hi):
        def body(j, carry):
            pos = j - jnp.where(j >= 2, 2, 0)
            use = jnp.where(j == 0, keep_first, jnp.where(j == 2, 1, jnp.where(j == 4, keep_fifth, hr)))
            halves = [work[pos], work[pos + 1]]
            full = jnp.concatenate(halves, 1)
            hi_part = full.astype(jnp.bfloat16)
            lo_part = (full - hi_part.astype(jnp.float32)).astype(jnp.bfloat16)
            both = jnp.concatenate([hi_part, lo_part], 0)
            rows = full.shape[0]
            for n in range(2):
                wh = whi[j, :, :, n * half:(n + 1) * half].reshape(wide, half)
                wl = wlo[j, :, :, n * half:(n + 1) * half].reshape(wide, half)
                big = jnp.dot(both, wh, preferred_element_type=jnp.float32)
                small = jnp.dot(hi_part, wl, preferred_element_type=jnp.float32)
                result = big[:rows] + (big[rows:] + small)
                work[pos + n] = jnp.where(use > 0, result, halves[n])
            return carry

        lax.fori_loop(lo, hi, body, 0)

    has_b = has_left
    first = place == 0
    total = jnp.where(has_b, 5, 2)
    split_at = jnp.where(first, 2, 5)
    for step in (step_one, step_two, step_three):
        each(step, 0, split_at)
    later = jnp.maximum(total, split_at)
    each(step_one, split_at, later)
    each(step_four, 0, split_at)
    each(step_five, 0, split_at)

    @pl.when(jnp.logical_not(has_right))
    def _():
        right1[...] = jnp.zeros(right1.shape, jnp.float32)

    def arrived(dst, landing):
        vcopy(dst, dst, 0, landing, col).wait_recv()

    @pl.when(first)
    def _():
        one[0] = own[0]
        one[1] = own[1]

        arrived(right1.at[0], 0)
        one[2] = right1[0]

    @pl.when(place == 1)
    def _():
        @pl.when(has_right)
        def _():
            arrived(right1, 0)

        one[1] = own[1]
        one[2] = right1[0]
        one[3] = right1[1]
        arrived(left.at[0], 2)
        one[0] = left[0]

    @pl.when(place == 2)
    def _():
        arrived(right1, 0)
        one[2] = right1[0]
        one[3] = right1[1]
        arrived(left.at[1], 3)
        one[1] = left[1]
        arrived(left.at[0], 2)
        one[0] = left[0]

    products(one, jnp.where(first, 0, 2), jnp.where(first, 2, 5))

    def first_half_right(work):
        return vcopy(work.at[2], left.at[0], 1, 2, col + 1)

    def second_half_right():
        return vcopy(one.at[3], left.at[1], 2, 3, col + 1)

    def early_left():
        return vcopy(one.at[pl.ds(0, 2)], right1, 3, 0, col - 1)

    def late_left():
        return vcopy(two.at[pl.ds(0, 2)], right2, 3, 1, col - 1)

    def last_right():
        return vcopy(two.at[pl.ds(2, 2)], last, 4, 4, col + 1)

    @pl.when(first)
    def _():
        @pl.when(has_right)
        def _():
            first_half_right(one).start()

        @pl.when(has_left)
        def _():
            early_left().start()

    @pl.when(jnp.logical_and(place > 0, has_right))
    def _():
        second_half_right().start()

    for step in (step_two, step_three, step_four, step_five):
        each(step, split_at, later)

    @pl.when(jnp.logical_and(first, has_b))
    def _():
        @pl.when(has_right)
        def _():
            arrived(right2, 1)

        two[2] = right2[0]
        two[3] = right2[1]
        arrived(left.at[1], 3)
        two[1] = left[1]
        arrived(left.at[0], 2)
        two[0] = left[0]

    @pl.when(place > 0)
    def _():
        two[0] = one[0]
        two[1] = one[1]
        two[2] = one[2]

    products(two, jnp.where(first, 2, 0), jnp.where(first, total, 2))

    def give(ref):
        out[:, :half] = ref[0]
        out[:, half:] = ref[1]

    @pl.when(jnp.logical_and(first, has_b))
    def _():
        @pl.when(has_right)
        def _():
            last_right().start()

        give(two)

    @pl.when(col == 0)
    def _():
        give(one)

    @pl.when(place > 0)
    def _():
        @pl.when(has_right)
        def _():
            first_half_right(two).start()

    @pl.when(jnp.logical_and(place == 1, col > 1))
    def _():
        late_left().start()
        arrived(last, 4)
        give(last)

    @pl.when(jnp.logical_or(place == 2, col == 1))
    def _():
        give(two)

    @pl.when(has_right)
    def _():
        for i in range(3):
            hop_copy(i).wait_send()
        first_half_right(two).wait_send()

    @pl.when(place == 1)
    def _():
        loan_half().wait_send()

    @pl.when(place == 2)
    def _():
        loan_block().wait_send()

    @pl.when(jnp.logical_and(place > 0, has_right))
    def _():
        second_half_right().wait_send()

    @pl.when(jnp.logical_and(first, has_left))
    def _():
        early_left().wait_send()

        @pl.when(has_right)
        def _():
            last_right().wait_send()

    @pl.when(jnp.logical_and(place == 1, col > 1))
    def _():
        late_left().wait_send()

    def drain(f, carry):
        for slot in range(7):
            shard(f, chip, xnext, slot).wait_send()
        to_sibling(f).wait_send()
        return carry

    lax.fori_loop(0, total, drain, 0)


def on_device(vectors, factors, offsets):
    rows, cols = vectors.shape
    half = cols // 2
    depth = factors.shape[2]
    f32, dma = jnp.float32, pltpu.SemaphoreType.DMA
    in_vmem = pl.BlockSpec(memory_space=pltpu.VMEM)
    in_place = pl.BlockSpec(memory_space=pltpu.HBM)
    return pl.pallas_call(
        functools.partial(kernel, lax.axis_size("col")),
        out_shape=jax.ShapeDtypeStruct((rows, cols), f32),
        in_specs=[in_place, in_place, pl.BlockSpec(memory_space=pltpu.SMEM)],
        out_specs=in_vmem,
        scratch_shapes=[
            pltpu.VMEM((1, 4, depth, cols), f32),
            pltpu.VMEM((5, 8, 2, depth, cols), f32),
            pltpu.VMEM((3, depth, cols), f32),
            pltpu.VMEM((5, 16, depth, cols), jnp.bfloat16),
            pltpu.VMEM((5, 16, depth, cols), jnp.bfloat16),
            pltpu.VMEM((2, rows, half), f32),
            pltpu.VMEM((4, rows, half), f32),
            pltpu.VMEM((4, rows, half), f32),
            pltpu.VMEM((2, rows, half), f32),
            pltpu.VMEM((2, rows, half), f32),
            pltpu.VMEM((2, rows, half), f32),
            pltpu.VMEM((2, rows, half), f32),
            dma((5, 7)), dma((5, 8)), dma((5,)), dma((5,)), dma((3,)), dma((3,)), dma((5,)), dma((5,)), dma((3,)),
        ],
        compiler_params=pltpu.CompilerParams(
            collective_id=0, has_side_effects=True, vmem_limit_bytes=60 << 20),
    )(vectors, factors, offsets)


def solution(mesh):
    placed = (P("row", "col"), P("col", None, "row", None), P())
    return jax.shard_map(
        on_device, mesh=mesh, in_specs=placed, out_specs=P("row", "col"), check_vma=False
    )
```

```python
import functools

import jax
import jax.numpy as jnp
from jax import lax
from jax.experimental import pallas as pl
from jax.experimental.pallas import tpu as pltpu
from jax.sharding import PartitionSpec as P

MESH = pl.DeviceIdType.MESH
PARTS = 4


def kernel(groups, vec, fac, off, out, fetched, gather, hop, whi, wlo, own, one, two, right1, right2, left, last,
           gsend, grecv, ssend, srecv, zsend, zrecv, vsend, vrecv, fsem):
    row = lax.axis_index("row")
    col = lax.axis_index("col")
    half = own.shape[2]
    core = lax.rem(row, 2)
    chip = row // 2
    x = lax.rem(chip, 4)
    y = chip // 4
    place = lax.rem(col, 3)
    has_left = col > 0
    has_right = col < groups - 1
    xnext = y * 4 + lax.rem(x + 1, 4)
    xprev = y * 4 + lax.rem(x + 3, 4)
    xfar = y * 4 + lax.rem(x + 2, 4)
    other = (1 - y) * 4
    ychip = other + x
    sibling = chip * 2 + (1 - core)

    fetches = [
        pltpu.make_async_copy(fac, fetched, fsem.at[0]),
        pltpu.make_async_copy(vec.at[:, pl.ds(0, half)], own.at[0], fsem.at[1]),
        pltpu.make_async_copy(vec.at[:, pl.ds(half, half)], own.at[1], fsem.at[2]),
    ]
    for fetch in fetches:
        fetch.start()

    barrier = pltpu.get_barrier_semaphore()

    def greet(r, c):
        pl.semaphore_signal(barrier, inc=1, device_id=(r, c), device_id_type=MESH)

    for c in (xnext, xprev, ychip):
        greet(c * 2 + core, col)
    greet(sibling, col)

    @pl.when(has_left)
    def _():
        greet(row, col - 1)

    @pl.when(has_right)
    def _():
        greet(row, col + 1)

    for fetch in fetches:
        fetch.wait()
    for i in range(2):
        gather[i, chip, core] = fetched[0, i]
        hop[i] = fetched[0, i + 2]

    pl.semaphore_wait(barrier, 4 + has_left.astype(jnp.int32) + has_right.astype(jnp.int32))

    def hop_copy(i):
        return pltpu.make_async_remote_copy(
            hop.at[i], gather.at[i + 2, chip, core], zsend.at[i], zrecv.at[i],
            device_id=(row, col + 1), device_id_type=MESH)

    @pl.when(has_right)
    def _():
        for i in range(2):
            hop_copy(i).start()

    def vcopy(src, dst, slot, landing, to, part=0):
        return pltpu.make_async_remote_copy(
            src, dst, vsend.at[slot, part], vrecv.at[landing, part], device_id=(row, to), device_id_type=MESH)

    def loan_block():
        return vcopy(own, right1, 0, 0, col - 1)

    @pl.when(place > 0)
    def _():
        loan_block().start()

    def shard(f, s, to, slot):
        return pltpu.make_async_remote_copy(
            gather.at[f, s, core], gather.at[f, s, core], gsend.at[f, slot], grecv.at[f, s],
            device_id=(to * 2 + core, col), device_id_type=MESH)

    def got(f, s):
        shard(f, s, xnext, 0).wait_recv()

    def step_one(f):
        @pl.when(f >= 2)
        def _():
            hop_copy(f - 2).wait_recv()

        shard(f, chip, ychip, 0).start()
        shard(f, chip, xnext, 1).start()
        shard(f, chip, xprev, 2).start()

    def step_two(f):
        @pl.when(core == 0)
        def _():
            up = lax.rem(f, 2) == 0
            got(f, xprev)
            shard(f, xprev, ychip, 3).start()

            @pl.when(up)
            def _():
                shard(f, xprev, xnext, 4).start()

            got(f, xnext)
            shard(f, xnext, ychip, 5).start()

            @pl.when(jnp.logical_not(up))
            def _():
                shard(f, xnext, xprev, 4).start()

        @pl.when(core == 1)
        def _():
            got(f, ychip)
            shard(f, ychip, xnext, 3).start()
            shard(f, ychip, xprev, 4).start()
            got(f, xprev)
            shard(f, xprev, xnext, 5).start()

    def step_three(f):
        @pl.when(core == 0)
        def _():
            got(f, xfar)
            shard(f, xfar, ychip, 6).start()

        @pl.when(core == 1)
        def _():
            relayed = other + lax.rem(x + 1, 4)
            got(f, relayed)
            shard(f, relayed, xprev, 6).start()

    def to_sibling(f):
        return pltpu.make_async_remote_copy(
            gather.at[f, :, core], gather.at[f, :, core], ssend.at[f], srecv.at[f],
            device_id=(sibling, col), device_id_type=MESH)

    def from_sibling(f):
        return pltpu.make_async_remote_copy(
            gather.at[f, :, 1 - core], gather.at[f, :, 1 - core], ssend.at[f], srecv.at[f],
            device_id=(sibling, col), device_id_type=MESH)

    def step_four(f):
        @pl.when(core == 0)
        def _():
            for i in range(4):
                got(f, other + i)

        @pl.when(core == 1)
        def _():
            got(f, xnext)
            got(f, xfar)
            got(f, other + lax.rem(x + 2, 4))
            got(f, other + lax.rem(x + 3, 4))

        to_sibling(f).start()

    def step_five(f):
        from_sibling(f).wait_recv()

        def split(i, carry):
            for k in range(2):
                g = gather[f, i, k]
                hi = g.astype(jnp.bfloat16)
                whi[f, 2 * i + k] = hi
                wlo[f, 2 * i + k] = (g - hi.astype(jnp.float32)).astype(jnp.bfloat16)
            return carry

        lax.fori_loop(0, 8, split, 0)

    def each(step, lo, hi):
        def body(f, carry):
            step(f)
            return carry

        lax.fori_loop(lo, hi, body, 0)

    wide = 2 * half
    hr = has_right.astype(jnp.int32)

    def products(work, lo, hi, rows):
        def body(j, carry):
            k = lax.rem(j, 2)
            moved = off[jnp.where(j < 2, col, jnp.maximum(col - 1, 0))]
            use = jnp.where(k == 0, jnp.maximum(hr, 1 - moved), hr) > 0
            moved = moved > 0
            first, second, third = (work[k + n, rows, :] for n in range(3))
            halves = [jnp.where(moved, second, first), jnp.where(moved, third, second)]
            full = jnp.concatenate(halves, 1)
            hi_part = full.astype(jnp.bfloat16)
            lo_part = (full - hi_part.astype(jnp.float32)).astype(jnp.bfloat16)
            both = jnp.concatenate([hi_part, lo_part], 0)
            count = full.shape[0]
            results = []
            for n in range(2):
                wh = whi[j, :, :, n * half:(n + 1) * half].reshape(wide, half)
                wl = wlo[j, :, :, n * half:(n + 1) * half].reshape(wide, half)
                big = jnp.dot(both, wh, preferred_element_type=jnp.float32)
                small = jnp.dot(hi_part, wl, preferred_element_type=jnp.float32)
                results.append(jnp.where(use, big[:count] + (big[count:] + small), halves[n]))
            work[k, rows, :] = jnp.where(moved, first, results[0])
            work[k + 1, rows, :] = jnp.where(moved, results[0], results[1])
            work[k + 2, rows, :] = jnp.where(moved, results[1], third)
            return carry

        lax.fori_loop(lo, hi, body, 0)

    first = place == 0
    total = jnp.where(has_left, 4, 2)

    each(step_one, 0, 2)

    def second_round(f):
        step_two(f)

        @pl.when(place > 0)
        def _():
            step_one(f + 2)

    def third_round(f):
        step_three(f)

        @pl.when(place > 0)
        def _():
            step_two(f + 2)

    def fourth_round(f):
        step_three(f)
        step_four(f - 2)

        @pl.when(f > 2)
        def _():
            step_five(f - 3)

    def fifth_round(f):
        step_four(f)
        step_five(f - 1)

    each(second_round, 0, 2)

    each(third_round, 0, 2)

    @pl.when(place > 0)
    def _():
        each(fourth_round, 2, 4)
        each(fifth_round, 2, 4)
        step_five(3)

    @pl.when(first)
    def _():
        each(step_four, 0, 2)
        each(step_five, 0, 2)

    @pl.when(jnp.logical_not(has_right))
    def _():
        right1[...] = jnp.zeros(right1.shape, jnp.float32)
        right2[...] = jnp.zeros(right2.shape, jnp.float32)

    length = own.shape[1] // PARTS

    def rows_of(part):
        return pl.ds(pl.multiple_of(part * length, length), length)

    def arrived(dst, landing, part=0):
        vcopy(dst, dst, 0, landing, col, part).wait_recv()

    def left_back(part):
        arrived(left.at[:, rows_of(part)], 2, part)

    def block_right(part):
        return vcopy(one.at[pl.ds(2, 2), rows_of(part)], left.at[:, rows_of(part)], 1, 2, col + 1, part)

    def early_left():
        return vcopy(one.at[pl.ds(0, 2)], right1, 2, 0, col - 1)

    def late_left(part):
        return vcopy(one.at[pl.ds(0, 2), rows_of(part)], right2.at[:, rows_of(part)], 2, 1, col - 1, part)

    def last_right(part):
        return vcopy(two.at[pl.ds(2, 2), rows_of(part)], last.at[:, rows_of(part)], 3, 3, col + 1, part)

    lends_late = jnp.logical_and(place == 1, col > 1)

    @pl.when(has_right)
    def _():
        arrived(right1, 0)

    one[0] = own[0]
    one[1] = own[1]
    one[2] = right1[0]
    one[3] = right1[1]

    def first_stage(part):
        rows = rows_of(part)

        @pl.when(place > 0)
        def _():
            left_back(part)

            one[0, rows, :] = left[0, rows, :]
            one[1, rows, :] = left[1, rows, :]

            products(one, 2, 4, rows)

        products(one, 0, 2, rows)

        @pl.when(has_right)
        def _():
            block_right(part).start()

        @pl.when(lends_late)
        def _():
            late_left(part).start()

    each(first_stage, 0, PARTS)

    @pl.when(jnp.logical_and(first, has_left))
    def _():
        early_left().start()

        for step in (step_one, step_two, step_three, step_four, step_five):
            each(step, 2, total)

        def second_stage(part):
            rows = rows_of(part)

            @pl.when(has_right)
            def _():
                arrived(right2.at[:, rows], 1, part)

            left_back(part)
            two[0, rows, :] = left[0, rows, :]
            two[1, rows, :] = left[1, rows, :]
            two[2, rows, :] = right2[0, rows, :]
            two[3, rows, :] = right2[1, rows, :]
            products(two, 2, 4, rows)

            @pl.when(has_right)
            def _():
                last_right(part).start()

        each(second_stage, 0, PARTS)

    def give(ref):
        out[:, :half] = ref[0]
        out[:, half:] = ref[1]

    @pl.when(lends_late)
    def _():
        for part in range(PARTS):
            arrived(last.at[:, rows_of(part)], 3, part)
        give(last)

    @pl.when(jnp.logical_and(first, has_left))
    def _():
        give(two)

    @pl.when(jnp.logical_or(place == 2, col < 2))
    def _():
        give(one)

    @pl.when(has_right)
    def _():
        for i in range(2):
            hop_copy(i).wait_send()

    @pl.when(place > 0)
    def _():
        loan_block().wait_send()

    @pl.when(jnp.logical_and(first, has_left))
    def _():
        early_left().wait_send()

    def sent(part):
        @pl.when(has_right)
        def _():
            block_right(part).wait_send()

        @pl.when(lends_late)
        def _():
            late_left(part).wait_send()

        @pl.when(jnp.logical_and(jnp.logical_and(first, has_left), has_right))
        def _():
            last_right(part).wait_send()

    each(sent, 0, PARTS)

    def drain(f, carry):
        for slot in range(7):
            shard(f, chip, xnext, slot).wait_send()
        to_sibling(f).wait_send()
        return carry

    lax.fori_loop(0, total, drain, 0)


def on_device(vectors, factors, offsets):
    rows, cols = vectors.shape
    half = cols // 2
    depth = factors.shape[2]
    f32, dma = jnp.float32, pltpu.SemaphoreType.DMA
    in_vmem = pl.BlockSpec(memory_space=pltpu.VMEM)
    in_place = pl.BlockSpec(memory_space=pltpu.HBM)
    return pl.pallas_call(
        functools.partial(kernel, lax.axis_size("col")),
        out_shape=jax.ShapeDtypeStruct((rows, cols), f32),
        in_specs=[in_place, in_place, pl.BlockSpec(memory_space=pltpu.SMEM)],
        out_specs=in_vmem,
        scratch_shapes=[
            pltpu.VMEM((1, 4, depth, cols), f32),
            pltpu.VMEM((4, 8, 2, depth, cols), f32),
            pltpu.VMEM((2, depth, cols), f32),
            pltpu.VMEM((4, 16, depth, cols), jnp.bfloat16),
            pltpu.VMEM((4, 16, depth, cols), jnp.bfloat16),
            pltpu.VMEM((2, rows, half), f32),
            pltpu.VMEM((4, rows, half), f32),
            pltpu.VMEM((4, rows, half), f32),
            pltpu.VMEM((2, rows, half), f32),
            pltpu.VMEM((2, rows, half), f32),
            pltpu.VMEM((2, rows, half), f32),
            pltpu.VMEM((2, rows, half), f32),
            dma((4, 7)), dma((4, 8)), dma((4,)), dma((4,)), dma((2,)), dma((2,)),
            dma((4, PARTS)), dma((4, PARTS)), dma((3,)),
        ],
        compiler_params=pltpu.CompilerParams(
            collective_id=0, has_side_effects=True, vmem_limit_bytes=60 << 20),
    )(vectors, factors, offsets)


def solution(mesh):
    placed = (P("row", "col"), P("col", None, "row", None), P())
    return jax.shard_map(
        on_device, mesh=mesh, in_specs=placed, out_specs=P("row", "col"), check_vma=False
    )
```

```python
import functools

import jax
import jax.numpy as jnp
from jax import lax
from jax.experimental import pallas as pl
from jax.experimental.pallas import tpu as pltpu
from jax.sharding import PartitionSpec as P

MESH = pl.DeviceIdType.MESH
PARTS = 4


def kernel(groups, vec, fac, off, out, fetched, gather, hop, whi, wlo, own, one, two, right1, right2, left, last,
           gsend, grecv, ssend, srecv, zsend, zrecv, vsend, vrecv, fsem):
    row = lax.axis_index("row")
    col = lax.axis_index("col")
    half = own.shape[2]
    core = lax.rem(row, 2)
    chip = row // 2
    x = lax.rem(chip, 4)
    y = chip // 4
    place = lax.rem(col, 3)
    has_left = col > 0
    has_right = col < groups - 1
    xnext = y * 4 + lax.rem(x + 1, 4)
    xprev = y * 4 + lax.rem(x + 3, 4)
    xfar = y * 4 + lax.rem(x + 2, 4)
    other = (1 - y) * 4
    ychip = other + x
    sibling = chip * 2 + (1 - core)

    fetches = [
        pltpu.make_async_copy(fac, fetched, fsem.at[0]),
        pltpu.make_async_copy(vec.at[:, pl.ds(0, half)], own.at[0], fsem.at[1]),
        pltpu.make_async_copy(vec.at[:, pl.ds(half, half)], own.at[1], fsem.at[2]),
    ]
    for fetch in fetches:
        fetch.start()

    barrier = pltpu.get_barrier_semaphore()

    def greet(r, c):
        pl.semaphore_signal(barrier, inc=1, device_id=(r, c), device_id_type=MESH)

    for c in (xnext, xprev, ychip):
        greet(c * 2 + core, col)
    greet(sibling, col)

    @pl.when(has_left)
    def _():
        greet(row, col - 1)

    @pl.when(has_right)
    def _():
        greet(row, col + 1)

    for fetch in fetches:
        fetch.wait()
    for i in range(2):
        gather[i, chip, core] = fetched[0, i]
        hop[i] = fetched[0, i + 2]

    pl.semaphore_wait(barrier, 4 + has_left.astype(jnp.int32) + has_right.astype(jnp.int32))

    def hop_copy(i):
        return pltpu.make_async_remote_copy(
            hop.at[i], gather.at[i + 2, chip, core], zsend.at[i], zrecv.at[i],
            device_id=(row, col + 1), device_id_type=MESH)

    @pl.when(has_right)
    def _():
        for i in range(2):
            hop_copy(i).start()

    def vcopy(src, dst, slot, landing, to, part=0):
        return pltpu.make_async_remote_copy(
            src, dst, vsend.at[slot, part], vrecv.at[landing, part], device_id=(row, to), device_id_type=MESH)

    length = own.shape[1] // PARTS

    def rows_of(part):
        return pl.ds(pl.multiple_of(part * length, length), length)

    def loan_block(part):
        return vcopy(own.at[:, rows_of(part)], right1.at[:, rows_of(part)], 0, 0, col - 1, part)

    @pl.when(place > 0)
    def _():
        for part in range(PARTS):
            loan_block(part).start()

    def shard(f, s, to, slot):
        return pltpu.make_async_remote_copy(
            gather.at[f, s, core], gather.at[f, s, core], gsend.at[f, slot], grecv.at[f, s],
            device_id=(to * 2 + core, col), device_id_type=MESH)

    def to_sibling(f, s):
        return pltpu.make_async_remote_copy(
            gather.at[f, s, core], gather.at[f, s, core], ssend.at[f, s], srecv.at[f, s],
            device_id=(sibling, col), device_id_type=MESH)

    def from_sibling(f, s):
        return pltpu.make_async_remote_copy(
            gather.at[f, s, 1 - core], gather.at[f, s, 1 - core], ssend.at[f, s], srecv.at[f, s],
            device_id=(sibling, col), device_id_type=MESH)

    def got(f, s):
        shard(f, s, xnext, 0).wait_recv()
        to_sibling(f, s).start()

    def step_one(f):
        @pl.when(f >= 2)
        def _():
            hop_copy(f - 2).wait_recv()

        shard(f, chip, ychip, 0).start()
        shard(f, chip, xnext, 1).start()
        shard(f, chip, xprev, 2).start()
        to_sibling(f, chip).start()

    def step_two(f):
        @pl.when(core == 0)
        def _():
            up = lax.rem(f, 2) == 0
            got(f, xprev)
            shard(f, xprev, ychip, 3).start()

            @pl.when(up)
            def _():
                shard(f, xprev, xnext, 4).start()

            got(f, xnext)
            shard(f, xnext, ychip, 5).start()

            @pl.when(jnp.logical_not(up))
            def _():
                shard(f, xnext, xprev, 4).start()

        @pl.when(core == 1)
        def _():
            got(f, ychip)
            shard(f, ychip, xnext, 3).start()
            shard(f, ychip, xprev, 4).start()
            got(f, xprev)
            shard(f, xprev, xnext, 5).start()

    def step_three(f):
        @pl.when(core == 0)
        def _():
            got(f, xfar)
            shard(f, xfar, ychip, 6).start()

        @pl.when(core == 1)
        def _():
            relayed = other + lax.rem(x + 1, 4)
            got(f, relayed)
            shard(f, relayed, xprev, 6).start()

    def step_four(f):
        @pl.when(core == 0)
        def _():
            for i in range(4):
                got(f, other + i)

        @pl.when(core == 1)
        def _():
            got(f, xnext)
            got(f, xfar)
            got(f, other + lax.rem(x + 2, 4))
            got(f, other + lax.rem(x + 3, 4))

    def step_five(f):
        def split(i, carry):
            from_sibling(f, i).wait_recv()
            for k in range(2):
                g = gather[f, i, k]
                hi = g.astype(jnp.bfloat16)
                whi[f, 2 * i + k] = hi
                wlo[f, 2 * i + k] = (g - hi.astype(jnp.float32)).astype(jnp.bfloat16)
            return carry

        lax.fori_loop(0, 8, split, 0)

    def each(step, lo, hi):
        def body(f, carry):
            step(f)
            return carry

        lax.fori_loop(lo, hi, body, 0)

    wide = 2 * half
    hr = has_right.astype(jnp.int32)

    def products(work, lo, hi, rows):
        def body(j, carry):
            k = lax.rem(j, 2)
            moved = off[jnp.where(j < 2, col, jnp.maximum(col - 1, 0))]
            use = jnp.where(k == 0, jnp.maximum(hr, 1 - moved), hr) > 0
            moved = moved > 0
            first, second, third = (work[k + n, rows, :] for n in range(3))
            halves = [jnp.where(moved, second, first), jnp.where(moved, third, second)]
            full = jnp.concatenate(halves, 1)
            hi_part = full.astype(jnp.bfloat16)
            lo_part = (full - hi_part.astype(jnp.float32)).astype(jnp.bfloat16)
            both = jnp.concatenate([hi_part, lo_part], 0)
            count = full.shape[0]
            results = []
            for n in range(2):
                wh = whi[j, :, :, n * half:(n + 1) * half].reshape(wide, half)
                wl = wlo[j, :, :, n * half:(n + 1) * half].reshape(wide, half)
                big = jnp.dot(both, wh, preferred_element_type=jnp.float32)
                small = jnp.dot(hi_part, wl, preferred_element_type=jnp.float32)
                results.append(jnp.where(use, big[:count] + (big[count:] + small), halves[n]))
            work[k, rows, :] = jnp.where(moved, first, results[0])
            work[k + 1, rows, :] = jnp.where(moved, results[0], results[1])
            work[k + 2, rows, :] = jnp.where(moved, results[1], third)
            return carry

        lax.fori_loop(lo, hi, body, 0)

    first = place == 0
    total = jnp.where(has_left, 4, 2)

    each(step_one, 0, 2)

    def second_round(f):
        step_two(f)

        @pl.when(place > 0)
        def _():
            step_one(f + 2)

    def third_round(f):
        step_three(f)

        @pl.when(place > 0)
        def _():
            step_two(f + 2)

    def fourth_round(f):
        step_three(f)
        step_four(f - 2)

        @pl.when(f > 2)
        def _():
            step_five(f - 3)

    def fifth_round(f):
        step_four(f)
        step_five(f - 1)

    each(second_round, 0, 2)

    each(third_round, 0, 2)

    @pl.when(place > 0)
    def _():
        each(fourth_round, 2, 4)
        each(fifth_round, 2, 4)
        step_five(3)

    @pl.when(first)
    def _():
        each(step_four, 0, 2)
        each(step_five, 0, 2)

    @pl.when(jnp.logical_not(has_right))
    def _():
        right1[...] = jnp.zeros(right1.shape, jnp.float32)
        right2[...] = jnp.zeros(right2.shape, jnp.float32)

    def arrived(dst, landing, part=0):
        vcopy(dst, dst, 0, landing, col, part).wait_recv()

    def left_back(part):
        arrived(left.at[:, rows_of(part)], 2, part)

    def block_right(part):
        return vcopy(one.at[pl.ds(2, 2), rows_of(part)], left.at[:, rows_of(part)], 1, 2, col + 1, part)

    def early_left(part):
        return vcopy(one.at[pl.ds(0, 2), rows_of(part)], right1.at[:, rows_of(part)], 2, 0, col - 1, part)

    def late_left(part):
        return vcopy(one.at[pl.ds(0, 2), rows_of(part)], right2.at[:, rows_of(part)], 2, 1, col - 1, part)

    def last_right(part):
        return vcopy(two.at[pl.ds(2, 2), rows_of(part)], last.at[:, rows_of(part)], 3, 3, col + 1, part)

    lends_late = jnp.logical_and(place == 1, col > 1)

    one[0] = own[0]
    one[1] = own[1]

    def first_stage(part):
        rows = rows_of(part)

        @pl.when(has_right)
        def _():
            arrived(right1.at[:, rows], 0, part)

        one[2, rows, :] = right1[0, rows, :]
        one[3, rows, :] = right1[1, rows, :]

        @pl.when(place > 0)
        def _():
            left_back(part)

            one[0, rows, :] = left[0, rows, :]
            one[1, rows, :] = left[1, rows, :]

            products(one, 2, 4, rows)

        products(one, 0, 2, rows)

        @pl.when(has_right)
        def _():
            block_right(part).start()

        @pl.when(lends_late)
        def _():
            late_left(part).start()

    each(first_stage, 0, PARTS)

    @pl.when(jnp.logical_and(first, has_left))
    def _():
        for part in range(PARTS):
            early_left(part).start()

        for step in (step_one, step_two, step_three, step_four, step_five):
            each(step, 2, total)

        def second_stage(part):
            rows = rows_of(part)

            @pl.when(has_right)
            def _():
                arrived(right2.at[:, rows], 1, part)

            left_back(part)
            two[0, rows, :] = left[0, rows, :]
            two[1, rows, :] = left[1, rows, :]
            two[2, rows, :] = right2[0, rows, :]
            two[3, rows, :] = right2[1, rows, :]
            products(two, 2, 4, rows)

            @pl.when(has_right)
            def _():
                last_right(part).start()

        each(second_stage, 0, PARTS)

    def give(ref):
        out[:, :half] = ref[0]
        out[:, half:] = ref[1]

    @pl.when(lends_late)
    def _():
        for part in range(PARTS):
            arrived(last.at[:, rows_of(part)], 3, part)
        give(last)

    @pl.when(jnp.logical_and(first, has_left))
    def _():
        give(two)

    @pl.when(jnp.logical_or(place == 2, col < 2))
    def _():
        give(one)

    @pl.when(has_right)
    def _():
        for i in range(2):
            hop_copy(i).wait_send()

    def sent(part):
        @pl.when(place > 0)
        def _():
            loan_block(part).wait_send()

        @pl.when(jnp.logical_and(first, has_left))
        def _():
            early_left(part).wait_send()

        @pl.when(has_right)
        def _():
            block_right(part).wait_send()

        @pl.when(lends_late)
        def _():
            late_left(part).wait_send()

        @pl.when(jnp.logical_and(jnp.logical_and(first, has_left), has_right))
        def _():
            last_right(part).wait_send()

    each(sent, 0, PARTS)

    def drain(f, carry):
        for slot in range(7):
            shard(f, chip, xnext, slot).wait_send()
        for s in range(8):
            to_sibling(f, s).wait_send()
        return carry

    lax.fori_loop(0, total, drain, 0)


def on_device(vectors, factors, offsets):
    rows, cols = vectors.shape
    half = cols // 2
    depth = factors.shape[2]
    f32, dma = jnp.float32, pltpu.SemaphoreType.DMA
    in_vmem = pl.BlockSpec(memory_space=pltpu.VMEM)
    in_place = pl.BlockSpec(memory_space=pltpu.HBM)
    return pl.pallas_call(
        functools.partial(kernel, lax.axis_size("col")),
        out_shape=jax.ShapeDtypeStruct((rows, cols), f32),
        in_specs=[in_place, in_place, pl.BlockSpec(memory_space=pltpu.SMEM)],
        out_specs=in_vmem,
        scratch_shapes=[
            pltpu.VMEM((1, 4, depth, cols), f32),
            pltpu.VMEM((4, 8, 2, depth, cols), f32),
            pltpu.VMEM((2, depth, cols), f32),
            pltpu.VMEM((4, 16, depth, cols), jnp.bfloat16),
            pltpu.VMEM((4, 16, depth, cols), jnp.bfloat16),
            pltpu.VMEM((2, rows, half), f32),
            pltpu.VMEM((4, rows, half), f32),
            pltpu.VMEM((4, rows, half), f32),
            pltpu.VMEM((2, rows, half), f32),
            pltpu.VMEM((2, rows, half), f32),
            pltpu.VMEM((2, rows, half), f32),
            pltpu.VMEM((2, rows, half), f32),
            dma((4, 7)), dma((4, 8)), dma((4, 8)), dma((4, 8)), dma((2,)), dma((2,)),
            dma((4, PARTS)), dma((4, PARTS)), dma((3,)),
        ],
        compiler_params=pltpu.CompilerParams(
            collective_id=0, has_side_effects=True, vmem_limit_bytes=60 << 20),
    )(vectors, factors, offsets)


def solution(mesh):
    placed = (P("row", "col"), P("col", None, "row", None), P())
    return jax.shard_map(
        on_device, mesh=mesh, in_specs=placed, out_specs=P("row", "col"), check_vma=False
    )
```

```python
import functools

import jax
import jax.numpy as jnp
from jax import lax
from jax.experimental import pallas as pl
from jax.experimental.pallas import tpu as pltpu
from jax.sharding import PartitionSpec as P

MESH = pl.DeviceIdType.MESH
PARTS = 4


def kernel(groups, vec, fac, off, out, fetched, gather, hop, whi, wlo, own, one, two, right1, right2, left, last,
           gsend, grecv, ssend, srecv, zsend, zrecv, vsend, vrecv, fsem):
    row = lax.axis_index("row")
    col = lax.axis_index("col")
    half = own.shape[2]
    core = lax.rem(row, 2)
    chip = row // 2
    x = lax.rem(chip, 4)
    y = chip // 4
    place = lax.rem(col, 3)
    has_left = col > 0
    has_right = col < groups - 1
    xnext = y * 4 + lax.rem(x + 1, 4)
    xprev = y * 4 + lax.rem(x + 3, 4)
    xfar = y * 4 + lax.rem(x + 2, 4)
    other = (1 - y) * 4
    ychip = other + x
    sibling = chip * 2 + (1 - core)

    fetches = [
        pltpu.make_async_copy(fac, fetched, fsem.at[0]),
        pltpu.make_async_copy(vec.at[:, pl.ds(0, half)], own.at[0], fsem.at[1]),
        pltpu.make_async_copy(vec.at[:, pl.ds(half, half)], own.at[1], fsem.at[2]),
    ]
    for fetch in fetches:
        fetch.start()

    barrier = pltpu.get_barrier_semaphore()

    def greet(r, c):
        pl.semaphore_signal(barrier, inc=1, device_id=(r, c), device_id_type=MESH)

    for c in (xnext, xprev, ychip):
        greet(c * 2 + core, col)
    greet(sibling, col)

    @pl.when(has_left)
    def _():
        greet(row, col - 1)

    @pl.when(has_right)
    def _():
        greet(row, col + 1)

    for fetch in fetches:
        fetch.wait()
    for i in range(2):
        gather[i, chip, core] = fetched[0, i]
        hop[i] = fetched[0, i + 2]

    pl.semaphore_wait(barrier, 4 + has_left.astype(jnp.int32) + has_right.astype(jnp.int32))

    def hop_copy(i):
        return pltpu.make_async_remote_copy(
            hop.at[i], gather.at[i + 2, chip, core], zsend.at[i], zrecv.at[i],
            device_id=(row, col + 1), device_id_type=MESH)

    @pl.when(has_right)
    def _():
        for i in range(2):
            hop_copy(i).start()

    def vcopy(src, dst, slot, landing, to, part=0):
        return pltpu.make_async_remote_copy(
            src, dst, vsend.at[slot, part], vrecv.at[landing, part], device_id=(row, to), device_id_type=MESH)

    length = own.shape[1] // PARTS

    def rows_of(part):
        return pl.ds(pl.multiple_of(part * length, length), length)

    def loan_block(part):
        return vcopy(own.at[:, rows_of(part)], right1.at[:, rows_of(part)], 0, 0, col - 1, part)

    @pl.when(place > 0)
    def _():
        for part in range(PARTS):
            loan_block(part).start()

    def shard(f, s, to, slot):
        return pltpu.make_async_remote_copy(
            gather.at[f, s, core], gather.at[f, s, core], gsend.at[f, slot], grecv.at[f, s],
            device_id=(to * 2 + core, col), device_id_type=MESH)

    def to_sibling(f, s):
        return pltpu.make_async_remote_copy(
            gather.at[f, s, core], gather.at[f, s, core], ssend.at[f, s], srecv.at[f, s],
            device_id=(sibling, col), device_id_type=MESH)

    def from_sibling(f, s):
        return pltpu.make_async_remote_copy(
            gather.at[f, s, 1 - core], gather.at[f, s, 1 - core], ssend.at[f, s], srecv.at[f, s],
            device_id=(sibling, col), device_id_type=MESH)

    def got(f, s):
        shard(f, s, xnext, 0).wait_recv()
        to_sibling(f, s).start()

    def step_one(f):
        @pl.when(f >= 2)
        def _():
            hop_copy(f - 2).wait_recv()

        shard(f, chip, ychip, 0).start()
        shard(f, chip, xnext, 1).start()
        shard(f, chip, xprev, 2).start()
        to_sibling(f, chip).start()

    def step_two(f):
        @pl.when(core == 0)
        def _():
            up = lax.rem(f, 2) == 0
            got(f, xprev)
            shard(f, xprev, ychip, 3).start()

            @pl.when(up)
            def _():
                shard(f, xprev, xnext, 4).start()

            got(f, xnext)
            shard(f, xnext, ychip, 5).start()

            @pl.when(jnp.logical_not(up))
            def _():
                shard(f, xnext, xprev, 4).start()

        @pl.when(core == 1)
        def _():
            got(f, ychip)
            shard(f, ychip, xnext, 3).start()
            shard(f, ychip, xprev, 4).start()
            got(f, xprev)
            shard(f, xprev, xnext, 5).start()

    def step_three(f):
        @pl.when(core == 0)
        def _():
            got(f, xfar)
            shard(f, xfar, ychip, 6).start()

        @pl.when(core == 1)
        def _():
            relayed = other + lax.rem(x + 1, 4)
            got(f, relayed)
            shard(f, relayed, xprev, 6).start()

    def step_four(f):
        @pl.when(core == 0)
        def _():
            for i in range(4):
                got(f, other + i)

        @pl.when(core == 1)
        def _():
            got(f, xnext)
            got(f, xfar)
            got(f, other + lax.rem(x + 2, 4))
            got(f, other + lax.rem(x + 3, 4))

    def step_five(f):
        def split(i, carry):
            from_sibling(f, i).wait_recv()
            for k in range(2):
                g = gather[f, i, k]
                hi = g.astype(jnp.bfloat16)
                whi[f, 2 * i + k] = hi
                wlo[f, 2 * i + k] = (g - hi.astype(jnp.float32)).astype(jnp.bfloat16)
            return carry

        lax.fori_loop(0, 8, split, 0)

    def each(step, lo, hi):
        def body(f, carry):
            step(f)
            return carry

        lax.fori_loop(lo, hi, body, 0)

    wide = 2 * half
    hr = has_right.astype(jnp.int32)

    def products(work, lo, hi, rows):
        def body(j, carry):
            k = lax.rem(j, 2)
            moved = off[jnp.where(j < 2, col, jnp.maximum(col - 1, 0))]
            use = jnp.where(k == 0, jnp.maximum(hr, 1 - moved), hr) > 0
            moved = moved > 0
            first, second, third = (work[k + n, rows, :] for n in range(3))
            halves = [jnp.where(moved, second, first), jnp.where(moved, third, second)]
            full = jnp.concatenate(halves, 1)
            hi_part = full.astype(jnp.bfloat16)
            lo_part = (full - hi_part.astype(jnp.float32)).astype(jnp.bfloat16)
            both = jnp.concatenate([hi_part, lo_part], 0)
            count = full.shape[0]
            results = []
            for n in range(2):
                wh = whi[j, :, :, n * half:(n + 1) * half].reshape(wide, half)
                wl = wlo[j, :, :, n * half:(n + 1) * half].reshape(wide, half)
                big = jnp.dot(both, wh, preferred_element_type=jnp.float32)
                small = jnp.dot(hi_part, wl, preferred_element_type=jnp.float32)
                results.append(jnp.where(use, big[:count] + (big[count:] + small), halves[n]))
            work[k, rows, :] = jnp.where(moved, first, results[0])
            work[k + 1, rows, :] = jnp.where(moved, results[0], results[1])
            work[k + 2, rows, :] = jnp.where(moved, results[1], third)
            return carry

        lax.fori_loop(lo, hi, body, 0)

    first = place == 0
    total = jnp.where(has_left, 4, 2)

    each(step_one, 0, 2)

    def second_round(f):
        step_two(f)

        @pl.when(place > 0)
        def _():
            step_one(f + 2)

    def third_round(f):
        step_three(f)

        @pl.when(place > 0)
        def _():
            step_two(f + 2)

    def fourth_round(f):
        step_three(f)
        step_four(f - 2)

        @pl.when(f > 2)
        def _():
            step_five(f - 3)

    def fifth_round(f):
        step_four(f)
        step_five(f - 1)

    each(second_round, 0, 2)

    each(third_round, 0, 2)

    @pl.when(place > 0)
    def _():
        each(fourth_round, 2, 4)
        each(fifth_round, 2, 4)
        step_five(3)

    @pl.when(first)
    def _():
        each(step_four, 0, 2)
        each(step_one, 2, total)
        each(step_five, 0, 2)

    @pl.when(jnp.logical_not(has_right))
    def _():
        right1[...] = jnp.zeros(right1.shape, jnp.float32)
        right2[...] = jnp.zeros(right2.shape, jnp.float32)

    def arrived(dst, landing, part=0):
        vcopy(dst, dst, 0, landing, col, part).wait_recv()

    def left_back(part):
        arrived(left.at[:, rows_of(part)], 2, part)

    def block_right(part):
        return vcopy(one.at[pl.ds(2, 2), rows_of(part)], left.at[:, rows_of(part)], 1, 2, col + 1, part)

    def early_left(part):
        return vcopy(one.at[pl.ds(0, 2), rows_of(part)], right1.at[:, rows_of(part)], 2, 0, col - 1, part)

    def late_left(part):
        return vcopy(one.at[pl.ds(0, 2), rows_of(part)], right2.at[:, rows_of(part)], 2, 1, col - 1, part)

    def last_right(part):
        return vcopy(two.at[pl.ds(2, 2), rows_of(part)], last.at[:, rows_of(part)], 3, 3, col + 1, part)

    lends_late = jnp.logical_and(place == 1, col > 1)

    one[0] = own[0]
    one[1] = own[1]

    def first_stage(part):
        rows = rows_of(part)

        @pl.when(has_right)
        def _():
            arrived(right1.at[:, rows], 0, part)

        one[2, rows, :] = right1[0, rows, :]
        one[3, rows, :] = right1[1, rows, :]

        @pl.when(place > 0)
        def _():
            left_back(part)

            one[0, rows, :] = left[0, rows, :]
            one[1, rows, :] = left[1, rows, :]

            products(one, 2, 4, rows)

        products(one, 0, 2, rows)

        @pl.when(lends_late)
        def _():
            late_left(part).start()

        @pl.when(has_right)
        def _():
            block_right(part).start()

    each(first_stage, 0, PARTS)

    @pl.when(jnp.logical_and(first, has_left))
    def _():
        for part in range(PARTS):
            early_left(part).start()

        for step in (step_two, step_three, step_four, step_five):
            each(step, 2, total)

        def second_stage(part):
            rows = rows_of(part)

            @pl.when(has_right)
            def _():
                arrived(right2.at[:, rows], 1, part)

            left_back(part)
            two[0, rows, :] = left[0, rows, :]
            two[1, rows, :] = left[1, rows, :]
            two[2, rows, :] = right2[0, rows, :]
            two[3, rows, :] = right2[1, rows, :]
            products(two, 2, 4, rows)

            @pl.when(has_right)
            def _():
                last_right(part).start()

        each(second_stage, 0, PARTS)

    def give(ref):
        out[:, :half] = ref[0]
        out[:, half:] = ref[1]

    @pl.when(lends_late)
    def _():
        for part in range(PARTS):
            arrived(last.at[:, rows_of(part)], 3, part)
        give(last)

    @pl.when(jnp.logical_and(first, has_left))
    def _():
        give(two)

    @pl.when(jnp.logical_or(place == 2, col < 2))
    def _():
        give(one)

    @pl.when(has_right)
    def _():
        for i in range(2):
            hop_copy(i).wait_send()

    def sent(part):
        @pl.when(place > 0)
        def _():
            loan_block(part).wait_send()

        @pl.when(jnp.logical_and(first, has_left))
        def _():
            early_left(part).wait_send()

        @pl.when(has_right)
        def _():
            block_right(part).wait_send()

        @pl.when(lends_late)
        def _():
            late_left(part).wait_send()

        @pl.when(jnp.logical_and(jnp.logical_and(first, has_left), has_right))
        def _():
            last_right(part).wait_send()

    each(sent, 0, PARTS)

    def drain(f, carry):
        for slot in range(7):
            shard(f, chip, xnext, slot).wait_send()
        for s in range(8):
            to_sibling(f, s).wait_send()
        return carry

    lax.fori_loop(0, total, drain, 0)


def on_device(vectors, factors, offsets):
    rows, cols = vectors.shape
    half = cols // 2
    depth = factors.shape[2]
    f32, dma = jnp.float32, pltpu.SemaphoreType.DMA
    in_vmem = pl.BlockSpec(memory_space=pltpu.VMEM)
    in_place = pl.BlockSpec(memory_space=pltpu.HBM)
    return pl.pallas_call(
        functools.partial(kernel, lax.axis_size("col")),
        out_shape=jax.ShapeDtypeStruct((rows, cols), f32),
        in_specs=[in_place, in_place, pl.BlockSpec(memory_space=pltpu.SMEM)],
        out_specs=in_vmem,
        scratch_shapes=[
            pltpu.VMEM((1, 4, depth, cols), f32),
            pltpu.VMEM((4, 8, 2, depth, cols), f32),
            pltpu.VMEM((2, depth, cols), f32),
            pltpu.VMEM((4, 16, depth, cols), jnp.bfloat16),
            pltpu.VMEM((4, 16, depth, cols), jnp.bfloat16),
            pltpu.VMEM((2, rows, half), f32),
            pltpu.VMEM((4, rows, half), f32),
            pltpu.VMEM((4, rows, half), f32),
            pltpu.VMEM((2, rows, half), f32),
            pltpu.VMEM((2, rows, half), f32),
            pltpu.VMEM((2, rows, half), f32),
            pltpu.VMEM((2, rows, half), f32),
            dma((4, 7)), dma((4, 8)), dma((4, 8)), dma((4, 8)), dma((2,)), dma((2,)),
            dma((4, PARTS)), dma((4, PARTS)), dma((3,)),
        ],
        compiler_params=pltpu.CompilerParams(
            collective_id=0, has_side_effects=True, vmem_limit_bytes=60 << 20),
    )(vectors, factors, offsets)


def solution(mesh):
    placed = (P("row", "col"), P("col", None, "row", None), P())
    return jax.shard_map(
        on_device, mesh=mesh, in_specs=placed, out_specs=P("row", "col"), check_vma=False
    )
```
